768 devices in a mesh: fsdp: 96 (over y_hi, z, core), col: 8 (over y_lo, x).
Axes of the slice: x: 4, y: 8 (y_hi: 4, y_lo: 2; y = y_hi * 2 + y_lo), z: 12, core: 2. Of those that a mesh axis runs over, the one named last changes fastest.
Arguments:
- grad: bfloat16 [7680, 18432], P('fsdp', 'col'), may hold values from -20 to 20
- basis: bfloat16 [7680, 512], P('fsdp', 'col'), may hold values from -0.25 to 0.25
- exp_avg: float32 [8, 2304, 512], P('col', 'fsdp'), may hold values from -6 to 6
- exp_avg_sq: float32 [8, 2304, 512], P('col', 'fsdp'), may hold values from 0.05 to 5
- step: int32 [1], replicated, may hold values from 1 to 8
Outputs:
- update: bfloat16 [7680, 18432], P('fsdp', 'col')
- new_avg: float32 [8, 2304, 512], P('col', 'fsdp')
- new_sq: float32 [8, 2304, 512], P('col', 'fsdp')
The draws below stay inside these ranges and needn't reach their ends.
All inputs are finite; a program needn't handle non-finite values.
Results may differ from the reference program's by a relative error of at most 0.0049.
Values may be sent and summed in bfloat16 or wider, within the bound.
No kernel may reach another device: no remote copies, remote signals or barrier semaphores. Data moves between devices by JAX's collectives and lax.ppermute only.
A program may use at most 32 MiB of HBM per device.

```python
import math
import jax
import jax.numpy as jnp
from jax import lax

R = 512
M = 7680
CG = 2304
N = 18432
N_COL = 8


def with_spikes(drawn, stream_key, source, target, blocks, factor):
    def block_of(axis_at):
        return (jnp.arange(drawn.shape[axis_at]) // (drawn.shape[axis_at] // blocks)).reshape((-1,) + (1,) * (drawn.ndim - 1 - axis_at))

    one_side = jax.random.permutation(stream_key, blocks)[block_of(target)]
    other_side = (block_of(target) + blocks // 2) % blocks
    return jnp.where((block_of(source) == one_side) | (block_of(source) == other_side), factor * drawn, drawn)


def steps_of(stream_key, dims, pieces, smallest, largest):
    gain, own = 1.0, jax.random.fold_in(stream_key, 6)
    for dim, shards_of in pieces:
        heights = jnp.exp(jax.random.uniform(jax.random.fold_in(own, dim), (shards_of,), jnp.float32, smallest / len(pieces), largest / len(pieces)))
        gain = gain * jnp.repeat(heights, dims[dim] // shards_of).reshape([-1 if axis == dim else 1 for axis in range(len(dims))])
    return gain


def gaussian(own_key, extent, deviation, bound, pieces=(), kind=jnp.bfloat16):
    values = jax.random.normal(own_key, extent, jnp.float32) * deviation
    if len(pieces) > 0:
        values = steps_of(own_key, extent, pieces, -0.22, 0.18) * values
    return jnp.clip(values, min=-bound, max=bound).astype(kind)


def gaussian_with(rng, shape, spread, bound, pieces, heavy, dtype=jnp.bfloat16):
    result = spread * jax.random.normal(rng, shape, jnp.float32)
    if pieces:
        result = result * steps_of(rng, shape, pieces, -0.22, 0.18)
    return jnp.clip(with_spikes(result, jax.random.fold_in(rng, 3), *heavy), -bound, bound).astype(dtype)


def setup_inputs(seed: int = 0) -> dict:
    splits = jax.random.split(jax.random.key(seed), 6)
    return {
        "grad": gaussian_with(splits[0], (M, N), 1.0, 20.0, ((0, 96), (1, 8)), (0, 1, 96, 4.75)),
        "basis": gaussian(splits[1], (M, R), R ** -0.5, 0.25, ((0, 96), (1, 8))),
        "exp_avg": gaussian(splits[2], (N_COL, CG, R), 1.0, 6.0, ((0, 8), (1, 96)), jnp.float32),
        "exp_avg_sq": jnp.clip(jnp.exp(math.log(5.0) - 4.6051702 * jax.random.uniform(splits[3], (N_COL, CG, R), jnp.float32) ** steps_of(splits[3], (N_COL, CG, R), ((0, 8), (1, 96)), -0.2, 0.2)), 0.05, 5.0),
        "step": jax.random.randint(splits[4], (1,), 1, 9).astype(jnp.int32),
    }


beta_one = 0.9
beta_two = 0.999
adam_eps = 1e-08

def reference(grad, basis, exp_avg, exp_avg_sq, step):
    low = lax.dot_general(grad, basis, (((0,), (0,)), ((), ())), preferred_element_type=jnp.float32)
    low = low.reshape(N_COL, CG, R)
    new_avg = beta_one * exp_avg + (1.0 - beta_one) * low
    new_sq = beta_two * exp_avg_sq + (1.0 - beta_two) * low * low
    count = step[0].astype(jnp.float32)
    first_fix = 1.0 - jnp.power(jnp.float32(beta_one), count)
    second_fix = 1.0 - jnp.power(jnp.float32(beta_two), count)
    normalized = (new_avg / first_fix / (jnp.sqrt(new_sq / second_fix) + adam_eps)).astype(jnp.bfloat16)
    normalized = normalized.reshape(N, R)
    update = lax.dot_general(basis, normalized, (((1,), (1,)), ((), ())), preferred_element_type=jnp.float32)
    return (update.astype(jnp.bfloat16), new_avg, new_sq)
```

```python
import jax
import jax.numpy as jnp
from jax import lax
from jax.sharding import PartitionSpec as P

beta_one = 0.9
beta_two = 0.999
adam_eps = 1e-08

FSDP = ("yh", "zh", "zl", "c")
COL = ("yl", "x")
INNER = ("yh", "zh")
OUTER = ("zl", "c")


def exchange(x, axes):
    return lax.all_to_all(x, axes, split_axis=0, concat_axis=0, tiled=True)


def to_all(x, count):
    return jnp.broadcast_to(x[None], (count,) + x.shape)


def adam_moments(low, exp_avg, exp_avg_sq, step):
    new_avg = beta_one * exp_avg + (1.0 - beta_one) * low
    new_sq = beta_two * exp_avg_sq + (1.0 - beta_two) * low * low
    count = step[0].astype(jnp.float32)
    first_fix = 1.0 - jnp.power(jnp.float32(beta_one), count)
    second_fix = 1.0 - jnp.power(jnp.float32(beta_two), count)
    normalized = (new_avg / first_fix / (jnp.sqrt(new_sq / second_fix) + adam_eps)).astype(
        jnp.bfloat16
    )
    return (new_avg, new_sq, normalized)


def local(grad, basis, exp_avg, exp_avg_sq, step):
    rows, cols = grad.shape
    part = basis.shape[1]
    own = exp_avg.shape[1]
    rank = exp_avg.shape[2]
    n_col = rank // part
    n_outer = 8
    n_inner = cols // own // n_outer
    wide = cols // n_inner
    tall = rows * n_inner
    half = tall // 2
    blocks = grad.reshape(rows, n_inner, wide).transpose(1, 0, 2)
    got = exchange(jnp.concatenate([blocks, to_all(basis, n_inner)], axis=2), INNER)
    got = got.reshape(tall, wide + part)
    piece = got[:, wide:]
    folded = jnp.concatenate([piece[:half], piece[half:]], axis=1)
    folded = exchange(to_all(folded, n_col), COL)
    full = jnp.concatenate(
        [
            folded[:, :, :part].transpose(1, 0, 2).reshape(half, rank),
            folded[:, :, part:].transpose(1, 0, 2).reshape(half, rank),
        ],
        axis=0,
    )
    partial = lax.dot_general(
        got[:, :wide], full, (((0,), (0,)), ((), ())), preferred_element_type=jnp.float32
    )
    sums = exchange(partial.astype(jnp.bfloat16).reshape(n_outer, own, rank), OUTER)
    low = jnp.sum(sums.astype(jnp.float32), axis=0)
    new_avg, new_sq, normalized = adam_moments(
        low.reshape(exp_avg.shape), exp_avg, exp_avg_sq, step
    )
    normalized = exchange(to_all(normalized[0], n_outer), OUTER).reshape(wide, rank)
    update = lax.dot_general(
        full, normalized, (((1,), (1,)), ((), ())), preferred_element_type=jnp.float32
    ).astype(jnp.bfloat16)
    update = update.reshape(n_inner, rows, wide)
    even = jnp.concatenate(
        [
            update[:, :, :128],
            jnp.concatenate([update[:, : rows // 2, 128:], update[:, rows // 2 :, 128:]], axis=2),
        ],
        axis=1,
    )
    even = exchange(even, INNER)
    tail = even[:, rows:]
    update = jnp.concatenate(
        [
            even[:, :rows],
            jnp.concatenate([tail[:, :, :64], tail[:, :, 64:]], axis=1),
        ],
        axis=2,
    )
    update = update.transpose(1, 0, 2).reshape(rows, cols)
    return (update, new_avg, new_sq)


def solution(mesh):
    split = jax.sharding.Mesh(mesh.devices.reshape(4, 3, 4, 2, 2, 4), FSDP + COL)
    return jax.shard_map(
        local,
        mesh=split,
        in_specs=(
            P(FSDP, COL),
            P(FSDP, COL),
            P(COL, FSDP, None),
            P(COL, FSDP, None),
            P(),
        ),
        out_specs=(P(FSDP, COL), P(COL, FSDP, None), P(COL, FSDP, None)),
        check_vma=False,
    )
```

```python
import jax
import jax.numpy as jnp
from jax import lax
from jax.sharding import PartitionSpec as P

beta_one = 0.9
beta_two = 0.999
adam_eps = 1e-08

FSDP = ("y", "z", "core")
COL = ("y_lo", "x")
INNER = ("y", "core")
OUTER = ("z",)
N_Y, N_Z, N_CORE = 4, 12, 2
N_INNER = N_Y * N_CORE
N_OUTER = N_Z
N_COL = 8
LANES = 128


def exchange(x, axes):
    return lax.all_to_all(x, axes, split_axis=0, concat_axis=0, tiled=True)


def to_all(x, count):
    return jnp.broadcast_to(x[None], (count,) + x.shape)


def local(grad, basis, exp_avg, exp_avg_sq, step):
    rows, cols = grad.shape
    part = basis.shape[1]
    own, rank = exp_avg.shape[1:]
    wide = cols // N_INNER
    tall = rows * N_INNER
    half = tall // 2
    count = step[0].astype(jnp.float32)
    first_fix = 1.0 - jnp.power(jnp.float32(beta_one), count)
    second_fix = 1.0 - jnp.power(jnp.float32(beta_two), count)
    grad, basis, first_fix, second_fix = lax.optimization_barrier(
        (grad, basis, first_fix, second_fix)
    )

    blocks = grad.reshape(rows, N_Y, N_Z, N_CORE, own).transpose(1, 3, 0, 2, 4)
    blocks = blocks.reshape(N_INNER, rows, wide)
    got = exchange(jnp.concatenate([blocks, to_all(basis, N_INNER)], axis=2), INNER)
    got = got.reshape(tall, wide + part)

    piece = got[:, wide:]
    folded = jnp.concatenate([piece[:half], piece[half:]], axis=1)
    folded = exchange(to_all(folded, N_COL), COL)
    full = jnp.concatenate(
        [
            folded[:, :, :part].transpose(1, 0, 2).reshape(half, rank),
            folded[:, :, part:].transpose(1, 0, 2).reshape(half, rank),
        ],
        axis=0,
    )

    partial = lax.dot_general(
        got[:, :wide], full, (((0,), (0,)), ((), ())), preferred_element_type=jnp.float32
    )
    sums = exchange(partial.astype(jnp.bfloat16).reshape(N_OUTER, own, rank), OUTER)
    low = jnp.sum(sums.astype(jnp.float32), axis=0).reshape(exp_avg.shape)
    new_avg = beta_one * exp_avg + (1.0 - beta_one) * low
    new_sq = beta_two * exp_avg_sq + (1.0 - beta_two) * low * low
    normalized = (new_avg / first_fix / (jnp.sqrt(new_sq / second_fix) + adam_eps)).astype(
        jnp.bfloat16
    )

    normalized = exchange(to_all(normalized[0], N_OUTER), OUTER).reshape(wide, rank)
    update = lax.dot_general(
        full, normalized, (((1,), (1,)), ((), ())), preferred_element_type=jnp.float32
    ).astype(jnp.bfloat16)
    update = update.reshape(N_INNER, rows, wide)
    narrow = wide - 2 * LANES
    folds = LANES // narrow
    deep = -(-rows // (8 * folds)) * 8
    tail = jnp.pad(update[:, :, 2 * LANES :], ((0, 0), (0, folds * deep - rows), (0, 0)))
    tail = [tail[:, deep * k : deep * (k + 1)] for k in range(folds)]
    packed = jnp.concatenate(
        [update[:, :, :LANES], update[:, :, LANES : 2 * LANES], jnp.concatenate(tail, axis=2)],
        axis=1,
    )
    packed = exchange(packed, INNER)
    tail = packed[:, 2 * rows :]
    tail = [tail[:, :, narrow * k : narrow * (k + 1)] for k in range(folds)]
    tail = jnp.concatenate(tail, axis=1)[:, :rows]
    update = jnp.concatenate([packed[:, :rows], packed[:, rows : 2 * rows], tail], axis=2)
    update = update.reshape(N_Y, N_CORE, rows, N_Z, own).transpose(2, 0, 3, 1, 4)
    return (update.reshape(rows, cols), new_avg, new_sq)


def solution(mesh):
    split = jax.sharding.Mesh(mesh.devices.reshape(N_Y, N_Z, N_CORE, 2, 4), FSDP + COL)
    return jax.shard_map(
        local,
        mesh=split,
        in_specs=(
            P(FSDP, COL),
            P(FSDP, COL),
            P(COL, FSDP, None),
            P(COL, FSDP, None),
            P(),
        ),
        out_specs=(P(FSDP, COL), P(COL, FSDP, None), P(COL, FSDP, None)),
        check_vma=False,
    )
```

```python
import math

import jax
import jax.numpy as jnp
from jax import lax
from jax.sharding import PartitionSpec as P

beta_one = 0.9
beta_two = 0.999
adam_eps = 1e-08

SIZES = {"ya": 2, "yb": 2, "za": 2, "zb": 6, "core": 2, "y_lo": 2, "xa": 2, "xb": 2}
FSDP = ("ya", "yb", "za", "zb", "core")
COL = ("y_lo", "xa", "xb")
INNER = ("ya", "yb", "core")
OUTER = ("zb", "za")
OWNERS = ("za", "zb")
LANES = 128


def sizes(axes):
    return tuple(SIZES[axis] for axis in axes)


def order(axes, wanted):
    return tuple(axes.index(axis) for axis in wanted)


N_INNER = math.prod(sizes(INNER))
N_OUTER = math.prod(sizes(OUTER))
N_COL = math.prod(sizes(COL))


def exchange(x, axes):
    return lax.all_to_all(x, axes, split_axis=0, concat_axis=0, tiled=True)


def to_all(x, count):
    return jnp.broadcast_to(x[None], (count,) + x.shape)


def local(grad, basis, exp_avg, exp_avg_sq, step):
    rows, cols = grad.shape
    part = basis.shape[1]
    own, rank = exp_avg.shape[1:]
    wide = cols // N_INNER
    tall = rows * N_INNER
    count = step[0].astype(jnp.float32)
    first_fix = 1.0 - jnp.power(jnp.float32(beta_one), count)
    second_fix = 1.0 - jnp.power(jnp.float32(beta_two), count)
    sent = to_all(basis, N_INNER)
    grad, sent, first_fix, second_fix = lax.optimization_barrier(
        (grad, sent, first_fix, second_fix)
    )

    blocks = grad.reshape((rows,) + sizes(FSDP) + (own,))
    blocks = blocks.transpose(order(("m",) + FSDP + ("k",), INNER + ("m",) + OUTER + ("k",)))
    blocks = blocks.reshape(N_INNER, rows, wide)
    got = exchange(jnp.concatenate([blocks, sent], axis=2), INNER)
    got = got.reshape(tall, wide + part)

    full = exchange(to_all(got[:, wide:].T, N_COL), COL).reshape(rank, tall)

    partial = lax.dot_general(
        got[:, :wide], full, (((0,), (1,)), ((), ())), preferred_element_type=jnp.float32
    )
    sums = exchange(partial.astype(jnp.bfloat16).reshape(N_OUTER, own, rank), OUTER)
    low = jnp.sum(sums.astype(jnp.float32), axis=0).reshape(exp_avg.shape)
    new_avg = beta_one * exp_avg + (1.0 - beta_one) * low
    new_sq = beta_two * exp_avg_sq + (1.0 - beta_two) * low * low
    normalized = (new_avg / first_fix / (jnp.sqrt(new_sq / second_fix) + adam_eps)).astype(
        jnp.bfloat16
    )

    normalized = exchange(to_all(normalized[0], N_OUTER), OWNERS).reshape(wide, rank)
    update = lax.dot_general(
        full, normalized, (((0,), (1,)), ((), ())), preferred_element_type=jnp.float32
    ).astype(jnp.bfloat16)
    update = update.reshape(N_INNER, rows, wide)
    narrow = wide - 2 * LANES
    folds = LANES // narrow
    deep = -(-rows // (8 * folds)) * 8
    tail = jnp.pad(update[:, :, 2 * LANES :], ((0, 0), (0, folds * deep - rows), (0, 0)))
    tail = [tail[:, deep * k : deep * (k + 1)] for k in range(folds)]
    packed = jnp.concatenate(
        [update[:, :, :LANES], update[:, :, LANES : 2 * LANES], jnp.concatenate(tail, axis=2)],
        axis=1,
    )
    packed = exchange(packed, INNER)
    tail = packed[:, 2 * rows :]
    tail = [tail[:, :, narrow * k : narrow * (k + 1)] for k in range(folds)]
    tail = jnp.concatenate(tail, axis=1)[:, :rows]
    update = jnp.concatenate([packed[:, :rows], packed[:, rows : 2 * rows], tail], axis=2)
    update = update.reshape(sizes(INNER) + (rows,) + sizes(OWNERS) + (own,))
    update = update.transpose(order(INNER + ("m",) + OWNERS + ("k",), ("m",) + FSDP + ("k",)))
    return (update.reshape(rows, cols), new_avg, new_sq)


def solution(mesh):
    split = jax.sharding.Mesh(mesh.devices.reshape(sizes(FSDP + COL)), FSDP + COL)
    return jax.shard_map(
        local,
        mesh=split,
        in_specs=(
            P(FSDP, COL),
            P(FSDP, COL),
            P(COL, FSDP, None),
            P(COL, FSDP, None),
            P(),
        ),
        out_specs=(P(FSDP, COL), P(COL, FSDP, None), P(COL, FSDP, None)),
        check_vma=False,
    )
```

```python
import math

import jax
import jax.numpy as jnp
from jax import lax
from jax.sharding import PartitionSpec as P

beta_one = 0.9
beta_two = 0.999
adam_eps = 1e-08

SIZES = {"ya": 2, "yb": 2, "za": 2, "zb": 6, "core": 2, "y_lo": 2, "xa": 2, "xb": 2}
FSDP = ("ya", "yb", "za", "zb", "core")
COL = ("y_lo", "xa", "xb")
INNER = ("ya", "yb", "core")
OUTER = ("zb", "za")
LANES = 128


def sizes(axes):
    return tuple(SIZES[axis] for axis in axes)


def order(axes, wanted):
    return tuple(axes.index(axis) for axis in wanted)


N_INNER = math.prod(sizes(INNER))
N_OUTER = math.prod(sizes(OUTER))
N_COL = math.prod(sizes(COL))


def exchange(x, axes):
    return lax.all_to_all(x, axes, split_axis=0, concat_axis=0, tiled=True)


def to_all(x, count):
    return jnp.broadcast_to(x[None], (count,) + x.shape)


def local(grad, basis, exp_avg, exp_avg_sq, step):
    rows, cols = grad.shape
    part = basis.shape[1]
    own, rank = exp_avg.shape[1:]
    wide = cols // N_INNER
    tall = rows * N_INNER
    count = step[0].astype(jnp.float32)
    first_fix = 1.0 - jnp.power(jnp.float32(beta_one), count)
    second_fix = 1.0 - jnp.power(jnp.float32(beta_two), count)
    sent = to_all(basis, N_INNER)
    grad, sent, first_fix, second_fix = lax.optimization_barrier(
        (grad, sent, first_fix, second_fix)
    )

    blocks = grad.reshape((rows,) + sizes(FSDP) + (own,))
    blocks = blocks.transpose(order(("m",) + FSDP + ("k",), INNER + ("m",) + OUTER + ("k",)))
    blocks = blocks.reshape(N_INNER, rows, wide)
    got = exchange(jnp.concatenate([blocks, sent], axis=2), INNER)
    got = got.reshape(tall, wide + part)

    full = exchange(to_all(got[:, wide:].T, N_COL), COL).reshape(rank, tall)

    partial = lax.dot_general(
        got[:, :wide], full, (((0,), (1,)), ((), ())), preferred_element_type=jnp.float32
    )
    sums = exchange(partial.astype(jnp.bfloat16).reshape(N_OUTER, own, rank), OUTER)
    low = jnp.sum(sums.astype(jnp.float32), axis=0).reshape(exp_avg.shape)
    new_avg = beta_one * exp_avg + (1.0 - beta_one) * low
    new_sq = beta_two * exp_avg_sq + (1.0 - beta_two) * low * low
    normalized = (new_avg / first_fix / (jnp.sqrt(new_sq / second_fix) + adam_eps)).astype(
        jnp.bfloat16
    )

    normalized = exchange(to_all(normalized[0], N_OUTER), OUTER).reshape(wide, rank)
    update = lax.dot_general(
        full, normalized, (((0,), (1,)), ((), ())), preferred_element_type=jnp.float32
    ).astype(jnp.bfloat16)
    update = update.reshape(N_INNER, rows, wide)
    narrow = wide - 2 * LANES
    folds = LANES // narrow
    deep = -(-rows // (8 * folds)) * 8
    tail = jnp.pad(update[:, :, 2 * LANES :], ((0, 0), (0, folds * deep - rows), (0, 0)))
    tail = [tail[:, deep * k : deep * (k + 1)] for k in range(folds)]
    packed = jnp.concatenate(
        [update[:, :, :LANES], update[:, :, LANES : 2 * LANES], jnp.concatenate(tail, axis=2)],
        axis=1,
    )
    packed = exchange(packed, INNER)
    tail = packed[:, 2 * rows :]
    tail = [tail[:, :, narrow * k : narrow * (k + 1)] for k in range(folds)]
    tail = jnp.concatenate(tail, axis=1)[:, :rows]
    update = jnp.concatenate([packed[:, :rows], packed[:, rows : 2 * rows], tail], axis=2)
    update = update.reshape(sizes(INNER) + (rows,) + sizes(OUTER) + (own,))
    update = update.transpose(order(INNER + ("m",) + OUTER + ("k",), ("m",) + FSDP + ("k",)))
    return (update.reshape(rows, cols), new_avg, new_sq)


def solution(mesh):
    split = jax.sharding.Mesh(mesh.devices.reshape(sizes(FSDP + COL)), FSDP + COL)
    return jax.shard_map(
        local,
        mesh=split,
        in_specs=(
            P(FSDP, COL),
            P(FSDP, COL),
            P(COL, FSDP, None),
            P(COL, FSDP, None),
            P(),
        ),
        out_specs=(P(FSDP, COL), P(COL, FSDP, None), P(COL, FSDP, None)),
        check_vma=False,
    )
```

```python
import math

import jax
import jax.numpy as jnp
from jax import lax
from jax.sharding import PartitionSpec as P

beta_one = 0.9
beta_two = 0.999
adam_eps = 1e-08

SIZES = {"ya": 2, "yb": 2, "za": 2, "zb": 6, "core": 2, "y_lo": 2, "xa": 2, "xb": 2}
FSDP = ("ya", "yb", "za", "zb", "core")
COL = ("y_lo", "xa", "xb")
INNER = ("yb", "ya", "core")
OUTER = ("zb", "za")
LANES = 128


def sizes(axes):
    return tuple(SIZES[axis] for axis in axes)


def order(axes, wanted):
    return tuple(axes.index(axis) for axis in wanted)


N_INNER = math.prod(sizes(INNER))
N_OUTER = math.prod(sizes(OUTER))
N_COL = math.prod(sizes(COL))


def exchange(x, axes):
    return lax.all_to_all(x, axes, split_axis=0, concat_axis=0, tiled=True)


def to_all(x, count):
    return jnp.broadcast_to(x[None], (count,) + x.shape)


def local(grad, basis, exp_avg, exp_avg_sq, step):
    rows, cols = grad.shape
    part = basis.shape[1]
    own, rank = exp_avg.shape[1:]
    wide = cols // N_INNER
    tall = rows * N_INNER
    count = step[0].astype(jnp.float32)
    first_fix = 1.0 - jnp.power(jnp.float32(beta_one), count)
    second_fix = 1.0 - jnp.power(jnp.float32(beta_two), count)
    sent = to_all(basis, N_INNER)
    grad, sent, first_fix, second_fix = lax.optimization_barrier(
        (grad, sent, first_fix, second_fix)
    )

    blocks = grad.reshape((rows,) + sizes(FSDP) + (own,))
    blocks = blocks.transpose(order(("m",) + FSDP + ("k",), INNER + ("m",) + OUTER + ("k",)))
    blocks = blocks.reshape(N_INNER, rows, wide)
    got = exchange(jnp.concatenate([blocks, sent], axis=2), INNER)
    got = got.reshape(tall, wide + part)

    full = exchange(to_all(got[:, wide:].T, N_COL), COL).reshape(rank, tall)

    partial = lax.dot_general(
        got[:, :wide], full, (((0,), (1,)), ((), ())), preferred_element_type=jnp.float32
    )
    sums = exchange(partial.astype(jnp.bfloat16).reshape(N_OUTER, own, rank), OUTER)
    low = jnp.sum(sums.astype(jnp.float32), axis=0).reshape(exp_avg.shape)
    new_avg = beta_one * exp_avg + (1.0 - beta_one) * low
    new_sq = beta_two * exp_avg_sq + (1.0 - beta_two) * low * low
    normalized = (new_avg / first_fix / (jnp.sqrt(new_sq / second_fix) + adam_eps)).astype(
        jnp.bfloat16
    )

    normalized = exchange(to_all(normalized[0], N_OUTER), OUTER).reshape(wide, rank)
    update = lax.dot_general(
        full, normalized, (((0,), (1,)), ((), ())), preferred_element_type=jnp.float32
    ).astype(jnp.bfloat16)
    update = update.reshape(N_INNER, rows, wide)
    narrow = wide - 2 * LANES
    folds = LANES // narrow
    deep = -(-rows // (8 * folds)) * 8
    tail = jnp.pad(update[:, :, 2 * LANES :], ((0, 0), (0, folds * deep - rows), (0, 0)))
    tail = [tail[:, deep * k : deep * (k + 1)] for k in range(folds)]
    packed = jnp.concatenate(
        [update[:, :, :LANES], update[:, :, LANES : 2 * LANES], jnp.concatenate(tail, axis=2)],
        axis=1,
    )
    packed = exchange(packed, INNER)
    tail = packed[:, 2 * rows :]
    tail = [tail[:, :, narrow * k : narrow * (k + 1)] for k in range(folds)]
    tail = jnp.concatenate(tail, axis=1)[:, :rows]
    update = jnp.concatenate([packed[:, :rows], packed[:, rows : 2 * rows], tail], axis=2)
    update = update.reshape(sizes(INNER) + (rows,) + sizes(OUTER) + (own,))
    update = update.transpose(order(INNER + ("m",) + OUTER + ("k",), ("m",) + FSDP + ("k",)))
    return (update.reshape(rows, cols), new_avg, new_sq)


def solution(mesh):
    split = jax.sharding.Mesh(mesh.devices.reshape(sizes(FSDP + COL)), FSDP + COL)
    return jax.shard_map(
        local,
        mesh=split,
        in_specs=(
            P(FSDP, COL),
            P(FSDP, COL),
            P(COL, FSDP, None),
            P(COL, FSDP, None),
            P(),
        ),
        out_specs=(P(FSDP, COL), P(COL, FSDP, None), P(COL, FSDP, None)),
        check_vma=False,
    )
```
